256 devices in a mesh: seq: 32 (over x, y, z_lo), head: 8 (over z_hi, core).
Axes of the slice: x: 4, y: 4, z: 8 (z_hi: 4, z_lo: 2; z = z_hi * 2 + z_lo), core: 2. Of those that a mesh axis runs over, the one named last changes fastest.
Arguments:
- queries: bfloat16 [36864, 5120], P(('seq', 'head')), may hold values from -120 to 120
- key_vectors: bfloat16 [36864, 5120], P(('seq', 'head')), may hold values from -20 to 20
- value_vectors: bfloat16 [36864, 5120], P(('seq', 'head')), may hold values from -6 to 6
- reach_time: int32 [96], P('seq'), may hold values from 0 to 1
- reach_width: int32 [96], P('seq'), may hold values from 0 to 2
- keep_mask: int32 [36864, 40], P('seq', 'head'), may hold values 0 or 1
Outputs:
- attended: bfloat16 [36864, 5120], P(('seq', 'head'))
The draws below stay inside these ranges and needn't reach their ends.
All inputs are finite; a program needn't handle non-finite values. No bound on the sum of `keep_mask` on one device may be relied on, other than what follows from the above.
Results may differ from the reference program's by a relative error of at most 0.0046.
Values may be sent and summed in bfloat16 or wider, within the bound.
A program may use at most 128 MiB of HBM per device.

```python
import math
import jax
import jax.numpy as jnp
from jax import lax

H = 40
HD = 128
TILE = 384
TILES_W = 3
TOKENS = 36864
NTILES = 96
N_SEQ = 32


def paired_draw(key):
    base_key = jax.random.fold_in(key, 11)
    first, second = jax.random.split(base_key, 2)
    width = H * HD
    query_draw = jnp.clip(jax.random.normal(first, (TOKENS, width), jnp.float32), -4.0, 4.0)
    key_draw = jnp.clip(jax.random.normal(second, (TOKENS, width), jnp.float32), -4.0, 4.0)
    return (query_draw, key_draw)


def draw_queries(key, part):
    return paired_draw(key)[0].astype(jnp.bfloat16)


def draw_key_vectors(key, part):
    return paired_draw(key)[1].astype(jnp.bfloat16)


def with_ends(drawn, own_key, least, top_value):
    longest = drawn.shape.index(max(drawn.shape))
    spots = []
    for shift in (0, 1):
        where = [jax.random.randint(jax.random.fold_in(own_key, axis), (), 0, length) for axis, length in enumerate(drawn.shape)]
        where[longest] = (where[longest] + shift) % drawn.shape[longest]
        spots.append(tuple(where))
    return drawn.at[spots[0]].set(least).at[spots[1]].set(top_value)


def level_of(stream_key, extent, cuts, least, largest):
    factor_of = 1.0
    for dim, parts in cuts:
        draws = jax.random.uniform(jax.random.fold_in(jax.random.fold_in(stream_key, 6), dim), (parts,), jnp.float32, least / len(cuts), largest / len(cuts))
        factor_of = factor_of * jnp.repeat(jnp.exp(draws), extent[dim] // parts).reshape((-1,) + (1,) * (len(extent) - 1 - dim))
    return factor_of


def scatter_about(stream_key, extent, spread, bound, shards=(), held_as=jnp.bfloat16):
    array = spread * jax.random.normal(stream_key, extent, jnp.float32)
    if shards:
        array = array * level_of(stream_key, extent, shards, -0.22, 0.18)
    return jnp.clip(array, -bound, bound).astype(held_as)


def setup_inputs(seed: int = 0) -> dict:
    splits = jax.random.split(jax.random.key(seed), 7)
    queries = draw_queries(jax.random.fold_in(splits[6], 71), 0)
    key_vectors = draw_key_vectors(jax.random.fold_in(splits[6], 71), 0)
    value_vectors = scatter_about(splits[2], (TOKENS, H * HD), 1.0, 6.0, ((0, 256),))
    reach_time = with_ends(jax.random.randint(splits[3], (NTILES,), 0, 2), jax.random.fold_in(splits[3], 1), 0, 1).astype(jnp.int32)
    reach_width = with_ends(jax.random.randint(splits[4], (NTILES,), 0, 3), jax.random.fold_in(splits[4], 1), 0, 2).astype(jnp.int32)
    keep_mask = with_ends((jax.random.randint(splits[5], (TOKENS, H), 0, 10) < 9).astype(jnp.int32), jax.random.fold_in(splits[5], 1), 0, 1)
    return dict(queries=queries, key_vectors=key_vectors, value_vectors=value_vectors, reach_time=reach_time, reach_width=reach_width, keep_mask=keep_mask)


def tile_mask(reach_t, reach_w, slab_index, slab_count):
    tile_count = reach_t.shape[0]
    places = jnp.arange(tile_count, dtype=jnp.int32)
    columns = jnp.arange(3 * tile_count, dtype=jnp.int32)
    offsets = columns // tile_count - 1
    key_place = columns % tile_count
    inside = (slab_index + offsets >= 0) & (slab_index + offsets < slab_count)
    near_time = jnp.abs(offsets)[None, :] <= reach_t[:, None]
    near_width = jnp.abs(key_place[None, :] - places[:, None]) <= reach_w[:, None]
    return near_time & near_width & inside[None, :]

def head_terms(query_head, key_head, value_head, allowed):
    tile_count = allowed.shape[0]
    slab_rows = query_head.shape[0]
    tile_rows = slab_rows // tile_count
    scores = jnp.dot(query_head.astype(jnp.float32), key_head.astype(jnp.float32).T, preferred_element_type=jnp.float32) * (1.0 / math.sqrt(query_head.shape[1]))
    scores = scores.reshape(tile_count, tile_rows, 3 * tile_count, tile_rows)
    mask_full = allowed[:, None, :, None]
    scores = jnp.where(mask_full, scores, -1e+30)
    highest = lax.optimization_barrier(jnp.max(scores, axis=(2, 3), keepdims=True))
    weights = jnp.where(mask_full, jnp.exp(scores - highest), 0.0)
    totals = lax.optimization_barrier(jnp.sum(weights, axis=(2, 3))).reshape(slab_rows)
    rounded = lax.optimization_barrier(weights.reshape(slab_rows, 3 * slab_rows).astype(jnp.bfloat16))
    summed = jnp.dot(rounded.astype(jnp.float32), value_head.astype(jnp.float32), preferred_element_type=jnp.float32)
    return (summed, totals)

def reference(queries, key_vectors, value_vectors, reach_time, reach_width, keep_mask):
    slab_rows = TILE * TILES_W
    query_slabs = queries.reshape(N_SEQ, slab_rows, H, HD)
    key_padded = jnp.pad(key_vectors.reshape(TOKENS, H, HD), ((slab_rows, slab_rows), (0, 0), (0, 0)))
    value_padded = jnp.pad(value_vectors.reshape(TOKENS, H, HD), ((slab_rows, slab_rows), (0, 0), (0, 0)))
    keep_slabs = keep_mask.reshape(N_SEQ, slab_rows, H)
    reach_t = reach_time.reshape(N_SEQ, TILES_W)
    reach_w = reach_width.reshape(N_SEQ, TILES_W)

    def one_slab(slab_index):
        allowed = tile_mask(reach_t[slab_index], reach_w[slab_index], slab_index, N_SEQ)
        key_rows = lax.dynamic_slice_in_dim(key_padded, slab_index * slab_rows, 3 * slab_rows, 0)
        value_rows = lax.dynamic_slice_in_dim(value_padded, slab_index * slab_rows, 3 * slab_rows, 0)
        query_heads = jnp.moveaxis(query_slabs[slab_index], 1, 0)
        key_heads = jnp.moveaxis(key_rows, 1, 0)
        value_heads = jnp.moveaxis(value_rows, 1, 0)

        def per_head(triple):
            return head_terms(triple[0], triple[1], triple[2], allowed)
        summed, totals = lax.map(per_head, (query_heads, key_heads, value_heads))
        factor = jnp.moveaxis(keep_slabs[slab_index], 1, 0).astype(jnp.float32) * (10.0 / 9.0)
        output = (summed * factor[:, :, None] / totals[:, :, None]).astype(jnp.bfloat16)
        return jnp.moveaxis(output, 0, 1)
    outputs = lax.map(one_slab, jnp.arange(N_SEQ, dtype=jnp.int32))
    return outputs.reshape(TOKENS, H * HD)
```

```python
import functools
import math

import jax
import jax.numpy as jnp
from jax import lax
from jax.experimental import pallas as pl
from jax.experimental.pallas import tpu as pltpu
from jax.sharding import PartitionSpec as P

MESH = pl.DeviceIdType.MESH
PLACES = 3
TILES = 3 * PLACES
PENALTY = 1e30


def kernel(
    group_heads, seq_count, head_count, compute,
    aux_ref, q_ref, k_ref, v_ref, o_ref,
    q_buf, k_buf, v_buf, o_buf, s_buf, p_buf, aux_buf,
    send_sem, near_sem, recv_sem, halo_send, halo_recv,
    out_send, out_near, out_recv, aux_send, aux_recv,
):
    rows, size = q_ref.shape[0], q_buf.shape[2]
    slab = q_buf.shape[1]
    tile = slab // PLACES
    columns = head_count
    scale = math.log2(math.e) / math.sqrt(size)

    seq, head = lax.axis_index("seq"), lax.axis_index("head")
    pair, low = seq // 2, seq % 2
    high, core = head // 2, head % 2
    here = high * 2 + low
    mine = pair * 2 + core
    is_self = low == core

    def at(z, of_core):
        return (pair * 2 + z % 2, (z // 2) * 2 + of_core)

    def beside(step):
        other = (mine + step + seq_count) % seq_count
        return ((other // 2) * 2 + low, high * 2 + other % 2)

    outside = beside(2 * core - 1)

    barrier = pltpu.get_barrier_semaphore()
    pl.semaphore_signal(barrier, inc=1, device_id=at(here, 1 - core), device_id_type=MESH)
    pl.semaphore_signal(barrier, inc=1, device_id=outside, device_id_type=MESH)

    def greet(step, carry):
        z = (here + step) % columns
        for of_core in range(2):
            pl.semaphore_signal(barrier, inc=1, device_id=at(z, of_core), device_id_type=MESH)
        return carry

    lax.fori_loop(1, columns, greet, 0)
    pl.semaphore_wait(barrier, 2 * columns)

    def aux_remote():
        return pltpu.make_async_remote_copy(
            src_ref=aux_ref, dst_ref=aux_buf, send_sem=aux_send, recv_sem=aux_recv,
            device_id=(pair * 2 + core, high * 2 + low), device_id_type=MESH,
        )

    @pl.when(is_self)
    def _():
        pltpu.make_async_copy(aux_ref, aux_buf, aux_recv).start()

    @pl.when(jnp.logical_not(is_self))
    def _():
        aux_remote().start()

    streams = ((k_ref, k_buf, 1), (v_ref, v_buf, 1), (q_ref, q_buf, 0))

    def landing(buf, offset, h):
        return buf.at[h, pl.ds(offset * slab, slab), :]

    def source(ref, z, h):
        return ref.at[:, pl.ds(pl.multiple_of((z * group_heads + h) * size, size), size)]

    def target(buf, offset, h):
        return buf.at[h, pl.ds(pl.multiple_of(offset * slab + head * rows, 16), rows), :]

    def send_head(h, carry):
        for t, (ref, buf, offset) in enumerate(streams):
            def send_to(step, inner, t=t, ref=ref, buf=buf, offset=offset):
                half = (step + 1) // 2
                z = (here + jnp.where(step % 2 == 1, half, columns - half)) % columns
                pltpu.make_async_remote_copy(
                    src_ref=source(ref, z, h), dst_ref=target(buf, offset, h),
                    send_sem=send_sem.at[t], recv_sem=recv_sem.at[t, h],
                    device_id=at(z, low), device_id_type=MESH,
                ).start()
                return inner

            lax.fori_loop(1, columns, send_to, 0)

            @pl.when(is_self)
            def _(t=t, ref=ref, buf=buf, offset=offset):
                pltpu.make_async_copy(source(ref, here, h), target(buf, offset, h), recv_sem.at[t, h]).start()

            @pl.when(jnp.logical_not(is_self))
            def _(t=t, ref=ref, buf=buf, offset=offset):
                pltpu.make_async_remote_copy(
                    src_ref=source(ref, here, h), dst_ref=target(buf, offset, h),
                    send_sem=near_sem.at[t], recv_sem=recv_sem.at[t, h],
                    device_id=at(here, low), device_id_type=MESH,
                ).start()
        return carry

    lax.fori_loop(0, group_heads, send_head, 0)

    def wait_for(ref, sem):
        pltpu.make_async_copy(ref, ref, sem).wait()

    def halo(t, side, h):
        buf = (k_buf, v_buf)[t]
        step = (-1, 1)[side]
        return pltpu.make_async_remote_copy(
            src_ref=landing(buf, 1, h), dst_ref=landing(buf, 1 - step, h),
            send_sem=halo_send.at[t, side, h], recv_sem=halo_recv.at[t, side, h],
            device_id=beside(step), device_id_type=MESH,
        )

    def take_head(h):
        for t, buf in enumerate((k_buf, v_buf)):
            wait_for(landing(buf, 1, h), recv_sem.at[t, h])
            for side in range(2):
                halo(t, side, h).start()

    def out_target(h):
        return o_ref.at[:, pl.ds(pl.multiple_of((here * group_heads + h) * size, size), size)]

    def send_out(h, block):
        src = o_buf.at[h, pl.ds(block * rows, rows), :]
        away = jnp.logical_or(core * columns + block != low * columns + head, False)

        @pl.when(jnp.logical_not(away))
        def _():
            pltpu.make_async_copy(src, out_target(h), out_recv).start()

        @pl.when(jnp.logical_and(away, block // 2 == high))
        def _():
            pltpu.make_async_remote_copy(
                src_ref=src, dst_ref=out_target(h), send_sem=out_near, recv_sem=out_recv,
                device_id=(pair * 2 + core, block), device_id_type=MESH,
            ).start()

        @pl.when(jnp.logical_and(away, block // 2 != high))
        def _():
            pltpu.make_async_remote_copy(
                src_ref=src, dst_ref=out_target(h), send_sem=out_send, recv_sem=out_recv,
                device_id=(pair * 2 + core, block), device_id_type=MESH,
            ).start()

    def attend(h, i):
        q = q_buf[h, i * tile:(i + 1) * tile, :]
        highest = jnp.full((tile, 128), -PENALTY, jnp.float32)
        for j in range(TILES):
            s = lax.dot_general(
                q, k_buf[h, j * tile:(j + 1) * tile, :], (((1,), (1,)), ((), ())),
                preferred_element_type=jnp.float32,
            )
            s_buf[:, j * tile:(j + 1) * tile] = s
            top = s[:, :128]
            for b in range(1, tile // 128):
                top = jnp.maximum(top, s[:, b * 128:(b + 1) * 128])
            highest = jnp.maximum(highest, top - aux_buf[5 + i:6 + i, j * 128:(j + 1) * 128])
        highest = jnp.max(highest, axis=1, keepdims=True) * scale
        total = jnp.zeros((tile, 128), jnp.float32)
        for j in range(TILES):
            level = highest + aux_buf[5 + i:6 + i, j * 128:(j + 1) * 128]
            for b in range(j * tile // 128, (j + 1) * tile // 128):
                w = jnp.exp2(s_buf[:, b * 128:(b + 1) * 128] * scale - level)
                total = total + w
                p_buf[:, b * 128:(b + 1) * 128] = w.astype(jnp.bfloat16)
        summed = jnp.dot(p_buf[...], v_buf[h], preferred_element_type=jnp.float32)
        total = jnp.sum(total, axis=1, keepdims=True)
        return summed, total

    def work_head(h):
        for t, buf in enumerate((k_buf, v_buf)):
            for side in range(2):
                halo(t, side, h).wait_recv()
        wait_for(landing(q_buf, 0, h), recv_sem.at[2, h])
        done = 0
        for i in range(PLACES):
            if compute:
                summed, total = attend(h, i)
                keep = aux_buf[pl.ds(h, 1), i * tile:(i + 1) * tile]
                keep = jnp.transpose(jnp.broadcast_to(keep, (8, tile)))[:, :1]
                o_buf[h, i * tile:(i + 1) * tile, :] = (summed * (keep / total)).astype(jnp.bfloat16)
            else:
                o_buf[h, i * tile:(i + 1) * tile, :] = q_buf[h, i * tile:(i + 1) * tile, :]
            ready = (i + 1) * tile // rows
            for block in range(done, ready):
                send_out(h, block)
            done = ready

    take_head(0)
    wait_for(aux_buf, aux_recv)

    def step(h, carry):
        take_head(h)
        work_head(h - 1)
        return carry

    lax.fori_loop(1, group_heads, step, 0)
    work_head(group_heads - 1)

    wait_for(o_ref, out_recv)
    far = (columns - 1) * group_heads * size
    near = group_heads * size
    for t, (ref, _, _) in enumerate(streams):
        wait_for(ref.at[:, :far], send_sem.at[t])

    @pl.when(jnp.logical_not(is_self))
    def _():
        aux_remote().wait_send()
        for t, (ref, _, _) in enumerate(streams):
            wait_for(ref.at[:, :near], near_sem.at[t])

    def settle(h, carry):
        for t in range(2):
            for side in range(2):
                halo(t, side, h).wait_send()
        return carry

    lax.fori_loop(0, group_heads, settle, 0)
    away_rows = (columns - 2) * rows
    wait_for(o_buf.at[:, pl.ds(0, away_rows), :], out_send)

    @pl.when(is_self)
    def _():
        wait_for(o_buf.at[:, pl.ds(0, rows), :], out_near)

    @pl.when(jnp.logical_not(is_self))
    def _():
        wait_for(o_buf.at[:, pl.ds(0, 2 * rows), :], out_near)


def tile_penalties(reach_t, reach_w, slab_index, slab_count):
    tile_count = reach_t.shape[0]
    places = jnp.arange(tile_count, dtype=jnp.int32)
    columns = jnp.arange(3 * tile_count, dtype=jnp.int32)
    offsets = columns // tile_count - 1
    key_place = columns % tile_count
    inside = (slab_index + offsets >= 0) & (slab_index + offsets < slab_count)
    near_time = jnp.abs(offsets)[None, :] <= reach_t[:, None]
    near_width = jnp.abs(key_place[None, :] - places[:, None]) <= reach_w[:, None]
    return jnp.where(near_time & near_width & inside[None, :], 0.0, PENALTY).astype(jnp.float32)


def on_device(compute, queries, key_vectors, value_vectors, reach_time, reach_width, keep_mask):
    seq_count, head_count = lax.axis_size("seq"), lax.axis_size("head")
    rows, width = queries.shape
    slab, group_heads = keep_mask.shape
    size = width // (group_heads * head_count)
    tile = slab // PLACES
    penalties = tile_penalties(reach_time, reach_width, lax.axis_index("seq"), seq_count)
    keep = keep_mask.astype(jnp.float32).T * (10.0 / 9.0)
    penalties = jnp.broadcast_to(penalties[:, :, None], (PLACES, TILES, 128)).reshape(PLACES, TILES * 128)
    wide = max(slab, TILES * 128)
    aux = jnp.concatenate([
        jnp.pad(keep, ((0, 0), (0, wide - slab))),
        jnp.pad(penalties, ((0, 0), (0, wide - TILES * 128))),
    ])
    hbm = pl.BlockSpec(memory_space=pl.ANY)
    vmem = pl.BlockSpec(memory_space=pltpu.VMEM)
    dma = pltpu.SemaphoreType.DMA
    bf16 = jnp.bfloat16
    return pl.pallas_call(
        functools.partial(kernel, group_heads, seq_count, head_count, compute),
        out_shape=jax.ShapeDtypeStruct((rows, width), bf16),
        in_specs=[vmem, hbm, hbm, hbm],
        out_specs=hbm,
        scratch_shapes=[
            pltpu.VMEM((group_heads, slab, size), bf16),
            pltpu.VMEM((group_heads, 3 * slab, size), bf16),
            pltpu.VMEM((group_heads, 3 * slab, size), bf16),
            pltpu.VMEM((group_heads, slab, size), bf16),
            pltpu.VMEM((tile, 3 * slab), jnp.float32),
            pltpu.VMEM((tile, 3 * slab), bf16),
            pltpu.VMEM(aux.shape, jnp.float32),
            dma((3,)), dma((3,)), dma((3, group_heads)),
            dma((2, 2, group_heads)), dma((2, 2, group_heads)),
            dma, dma, dma, dma, dma,
        ],
        compiler_params=pltpu.CompilerParams(
            collective_id=0, has_side_effects=True, vmem_limit_bytes=48 * 1024 * 1024
        ),
    )(aux, queries, key_vectors, value_vectors)


def solution(mesh, compute=True):
    return jax.shard_map(
        functools.partial(on_device, compute),
        mesh=mesh,
        in_specs=(
            P(("seq", "head"), None),
            P(("seq", "head"), None),
            P(("seq", "head"), None),
            P("seq"),
            P("seq"),
            P("seq", "head"),
        ),
        out_specs=P(("seq", "head"), None),
        check_vma=False,
    )
```

```python
import functools
import math

import jax
import jax.numpy as jnp
from jax import lax
from jax.experimental import pallas as pl
from jax.experimental.pallas import tpu as pltpu
from jax.sharding import PartitionSpec as P

MESH = pl.DeviceIdType.MESH
PLACES = 3
TILES = 3 * PLACES
PENALTY = 1e30


def kernel(
    group_heads, seq_count, head_count, compute,
    keep_ref, time_ref, width_ref, q_ref, k_ref, v_ref, o_ref,
    q_buf, k_buf, v_buf, o_buf, s_buf, p_buf, aux_ref, aux_buf,
    keep_buf, time_buf, width_buf, src_buf,
    send_sem, near_sem, recv_sem, halo_send, halo_recv,
    out_send, out_near, out_recv, aux_send, aux_recv, small_sem, src_sem,
):
    rows, size = q_ref.shape[0], q_buf.shape[2]
    slab = q_buf.shape[1]
    tile = slab // PLACES
    columns = head_count
    scale = math.log2(math.e) / math.sqrt(size)

    seq, head = lax.axis_index("seq"), lax.axis_index("head")
    pair, low = seq // 2, seq % 2
    high, core = head // 2, head % 2
    here = high * 2 + low
    mine = pair * 2 + core
    is_self = low == core

    def at(z, of_core):
        return (pair * 2 + z % 2, (z // 2) * 2 + of_core)

    def beside(step):
        other = (mine + step + seq_count) % seq_count
        return ((other // 2) * 2 + low, high * 2 + other % 2)

    outside = beside(2 * core - 1)

    loads = [
        pltpu.make_async_copy(src, src_buf.at[t], src_sem.at[t])
        for t, src in enumerate((k_ref, v_ref, q_ref))
    ]
    for copy in loads:
        copy.start()
    smalls = [
        pltpu.make_async_copy(src, dst, small_sem.at[n])
        for n, (src, dst) in enumerate(((keep_ref, keep_buf), (time_ref, time_buf), (width_ref, width_buf)))
    ]
    for copy in smalls:
        copy.start()

    barrier = pltpu.get_barrier_semaphore()
    pl.semaphore_signal(barrier, inc=1, device_id=at(here, 1 - core), device_id_type=MESH)
    pl.semaphore_signal(barrier, inc=1, device_id=outside, device_id_type=MESH)

    def greet(step, carry):
        z = (here + step) % columns
        for of_core in range(2):
            pl.semaphore_signal(barrier, inc=1, device_id=at(z, of_core), device_id_type=MESH)
        return carry

    lax.fori_loop(1, columns, greet, 0)
    pl.semaphore_wait(barrier, 2 * columns)

    def aux_remote():
        return pltpu.make_async_remote_copy(
            src_ref=aux_ref, dst_ref=aux_buf, send_sem=aux_send, recv_sem=aux_recv,
            device_id=(pair * 2 + core, high * 2 + low), device_id_type=MESH,
        )

    streams = ((src_buf.at[0], k_buf, 1), (src_buf.at[1], v_buf, 1), (src_buf.at[2], q_buf, 0))

    def landing(buf, offset, h):
        return buf.at[h, pl.ds(offset * slab, slab), :]

    def source(ref, z, h):
        return ref.at[:, pl.ds(pl.multiple_of((z * group_heads + h) * size, size), size)]

    def target(buf, offset, h):
        return buf.at[h, pl.ds(pl.multiple_of(offset * slab + head * rows, 16), rows), :]

    def send_head(h, carry):
        for t, (ref, buf, offset) in enumerate(streams):
            def send_to(step, inner, t=t, ref=ref, buf=buf, offset=offset):
                half = (step + 1) // 2
                z = (here + jnp.where(step % 2 == 1, half, columns - half)) % columns
                pltpu.make_async_remote_copy(
                    src_ref=source(ref, z, h), dst_ref=target(buf, offset, h),
                    send_sem=send_sem.at[t], recv_sem=recv_sem.at[t, h],
                    device_id=at(z, low), device_id_type=MESH,
                ).start()
                return inner

            lax.fori_loop(1, columns, send_to, 0)

            @pl.when(is_self)
            def _(t=t, ref=ref, buf=buf, offset=offset):
                pltpu.make_async_copy(source(ref, here, h), target(buf, offset, h), recv_sem.at[t, h]).start()

            @pl.when(jnp.logical_not(is_self))
            def _(t=t, ref=ref, buf=buf, offset=offset):
                pltpu.make_async_remote_copy(
                    src_ref=source(ref, here, h), dst_ref=target(buf, offset, h),
                    send_sem=near_sem.at[t], recv_sem=recv_sem.at[t, h],
                    device_id=at(here, low), device_id_type=MESH,
                ).start()
        return carry

    for copy in loads:
        copy.wait()
    lax.fori_loop(0, group_heads, send_head, 0)

    for copy in smalls:
        copy.wait()
    aux_ref[0:group_heads, :] = keep_buf[...].astype(jnp.float32) * (10.0 / 9.0)
    for i in range(PLACES):
        for j in range(TILES):
            offset, place = j // PLACES - 1, j % PLACES
            near = jnp.logical_and(abs(offset) <= time_buf[i], abs(place - i) <= width_buf[i])
            inside = jnp.logical_and(seq + offset >= 0, seq + offset < seq_count)
            penalty = jnp.where(jnp.logical_and(near, inside), 0.0, PENALTY).astype(jnp.float32)
            aux_ref[group_heads + i:group_heads + i + 1, j * 128:(j + 1) * 128] = jnp.full((1, 128), penalty)

    @pl.when(is_self)
    def _():
        pltpu.make_async_copy(aux_ref, aux_buf, aux_recv).start()

    @pl.when(jnp.logical_not(is_self))
    def _():
        aux_remote().start()

    def wait_for(ref, sem):
        pltpu.make_async_copy(ref, ref, sem).wait()

    def halo(t, side, h):
        buf = (k_buf, v_buf)[t]
        step = (-1, 1)[side]
        return pltpu.make_async_remote_copy(
            src_ref=landing(buf, 1, h), dst_ref=landing(buf, 1 - step, h),
            send_sem=halo_send.at[t, side, h], recv_sem=halo_recv.at[t, side, h],
            device_id=beside(step), device_id_type=MESH,
        )

    def take_head(h):
        for t, buf in enumerate((k_buf, v_buf)):
            wait_for(landing(buf, 1, h), recv_sem.at[t, h])
            for side in range(2):
                halo(t, side, h).start()

    def out_target(h):
        return o_ref.at[:, pl.ds(pl.multiple_of((here * group_heads + h) * size, size), size)]

    def send_out(h, block):
        src = o_buf.at[h, pl.ds(block * rows, rows), :]
        away = jnp.logical_or(core * columns + block != low * columns + head, False)

        @pl.when(jnp.logical_not(away))
        def _():
            pltpu.make_async_copy(src, out_target(h), out_recv).start()

        @pl.when(jnp.logical_and(away, block // 2 == high))
        def _():
            pltpu.make_async_remote_copy(
                src_ref=src, dst_ref=out_target(h), send_sem=out_near, recv_sem=out_recv,
                device_id=(pair * 2 + core, block), device_id_type=MESH,
            ).start()

        @pl.when(jnp.logical_and(away, block // 2 != high))
        def _():
            pltpu.make_async_remote_copy(
                src_ref=src, dst_ref=out_target(h), send_sem=out_send, recv_sem=out_recv,
                device_id=(pair * 2 + core, block), device_id_type=MESH,
            ).start()

    def attend(h, i):
        q = q_buf[h, i * tile:(i + 1) * tile, :]
        highest = jnp.full((tile, 128), -PENALTY, jnp.float32)
        for j in range(TILES):
            s = lax.dot_general(
                q, k_buf[h, j * tile:(j + 1) * tile, :], (((1,), (1,)), ((), ())),
                preferred_element_type=jnp.float32,
            )
            s_buf[:, j * tile:(j + 1) * tile] = s
            top = s[:, :128]
            for b in range(1, tile // 128):
                top = jnp.maximum(top, s[:, b * 128:(b + 1) * 128])
            highest = jnp.maximum(highest, top - aux_buf[group_heads + i:group_heads + i + 1, j * 128:(j + 1) * 128])
        highest = jnp.max(highest, axis=1, keepdims=True) * scale
        total = jnp.zeros((tile, 128), jnp.float32)
        for j in range(TILES):
            level = highest + aux_buf[group_heads + i:group_heads + i + 1, j * 128:(j + 1) * 128]
            for b in range(j * tile // 128, (j + 1) * tile // 128):
                w = jnp.exp2(s_buf[:, b * 128:(b + 1) * 128] * scale - level)
                total = total + w
                p_buf[:, b * 128:(b + 1) * 128] = w.astype(jnp.bfloat16)
        summed = jnp.dot(p_buf[...], v_buf[h], preferred_element_type=jnp.float32)
        total = jnp.sum(total, axis=1, keepdims=True)
        return summed, total

    def work_head(h):
        for t, buf in enumerate((k_buf, v_buf)):
            for side in range(2):
                halo(t, side, h).wait_recv()
        wait_for(landing(q_buf, 0, h), recv_sem.at[2, h])
        done = 0
        for i in range(PLACES):
            if compute:
                summed, total = attend(h, i)
                keep = aux_buf[pl.ds(h, 1), i * tile:(i + 1) * tile]
                keep = jnp.transpose(jnp.broadcast_to(keep, (8, tile)))[:, :1]
                o_buf[h, i * tile:(i + 1) * tile, :] = (summed * (keep / total)).astype(jnp.bfloat16)
            else:
                o_buf[h, i * tile:(i + 1) * tile, :] = q_buf[h, i * tile:(i + 1) * tile, :]
            ready = (i + 1) * tile // rows
            for block in range(done, ready):
                send_out(h, block)
            done = ready

    take_head(0)
    wait_for(aux_buf, aux_recv)

    def step(h, carry):
        take_head(h)
        work_head(h - 1)
        return carry

    lax.fori_loop(1, group_heads, step, 0)
    work_head(group_heads - 1)

    wait_for(o_ref, out_recv)
    far = (columns - 1) * group_heads * size
    near = group_heads * size
    for t, (ref, _, _) in enumerate(streams):
        wait_for(ref.at[:, :far], send_sem.at[t])

    @pl.when(jnp.logical_not(is_self))
    def _():
        aux_remote().wait_send()
        for t, (ref, _, _) in enumerate(streams):
            wait_for(ref.at[:, :near], near_sem.at[t])

    def settle(h, carry):
        for t in range(2):
            for side in range(2):
                halo(t, side, h).wait_send()
        return carry

    lax.fori_loop(0, group_heads, settle, 0)
    away_rows = (columns - 2) * rows
    wait_for(o_buf.at[:, pl.ds(0, away_rows), :], out_send)

    @pl.when(is_self)
    def _():
        wait_for(o_buf.at[:, pl.ds(0, rows), :], out_near)

    @pl.when(jnp.logical_not(is_self))
    def _():
        wait_for(o_buf.at[:, pl.ds(0, 2 * rows), :], out_near)


def on_device(compute, queries, key_vectors, value_vectors, reach_time, reach_width, keep_mask):
    seq_count, head_count = lax.axis_size("seq"), lax.axis_size("head")
    rows, width = queries.shape
    slab, group_heads = keep_mask.shape
    size = width // (group_heads * head_count)
    tile = slab // PLACES
    aux_shape = (group_heads + PLACES, max(slab, TILES * 128))
    hbm = pl.BlockSpec(memory_space=pltpu.HBM)
    dma = pltpu.SemaphoreType.DMA
    bf16 = jnp.bfloat16
    return pl.pallas_call(
        functools.partial(kernel, group_heads, seq_count, head_count, compute),
        out_shape=jax.ShapeDtypeStruct((rows, width), bf16),
        in_specs=[hbm] * 6,
        out_specs=pl.BlockSpec(memory_space=pltpu.VMEM),
        scratch_shapes=[
            pltpu.VMEM((group_heads, slab, size), bf16),
            pltpu.VMEM((group_heads, 3 * slab, size), bf16),
            pltpu.VMEM((group_heads, 3 * slab, size), bf16),
            pltpu.VMEM((group_heads, slab, size), bf16),
            pltpu.VMEM((tile, 3 * slab), jnp.float32),
            pltpu.VMEM((tile, 3 * slab), bf16),
            pltpu.VMEM(aux_shape, jnp.float32),
            pltpu.VMEM(aux_shape, jnp.float32),
            pltpu.VMEM((group_heads, slab), jnp.int32),
            pltpu.SMEM(reach_time.shape, jnp.int32),
            pltpu.SMEM(reach_width.shape, jnp.int32),
            pltpu.VMEM((3, rows, width), bf16),
            dma((3,)), dma((3,)), dma((3, group_heads)),
            dma((2, 2, group_heads)), dma((2, 2, group_heads)),
            dma, dma, dma, dma, dma, dma((3,)), dma((3,)),
        ],
        compiler_params=pltpu.CompilerParams(
            collective_id=0, has_side_effects=True, vmem_limit_bytes=48 * 1024 * 1024
        ),
    )(*(pltpu.with_memory_space_constraint(x, pltpu.HBM) for x in (keep_mask.T, reach_time, reach_width, queries, key_vectors, value_vectors)))


def solution(mesh, compute=True):
    return jax.shard_map(
        functools.partial(on_device, compute),
        mesh=mesh,
        in_specs=(
            P(("seq", "head"), None),
            P(("seq", "head"), None),
            P(("seq", "head"), None),
            P("seq"),
            P("seq"),
            P("seq", "head"),
        ),
        out_specs=P(("seq", "head"), None),
        check_vma=False,
    )
```

```python
import functools
import math

import jax
import jax.numpy as jnp
from jax import lax
from jax.experimental import pallas as pl
from jax.experimental.pallas import tpu as pltpu
from jax.sharding import PartitionSpec as P

MESH = pl.DeviceIdType.MESH
PLACES = 3
TILES = 3 * PLACES
PENALTY = 1e30


def kernel(
    group_heads, seq_count, head_count, compute,
    keep_ref, time_ref, width_ref, q_ref, k_ref, v_ref, o_ref,
    q_buf, k_buf, v_buf, o_buf, s_buf, p_buf, aux_ref, aux_buf,
    keep_buf, time_buf, width_buf,
    send_sem, near_sem, recv_sem, halo_send, halo_recv,
    out_send, out_near, out_recv, aux_send, aux_recv, small_sem,
):
    rows, size = q_ref.shape[0], q_buf.shape[2]
    slab = q_buf.shape[1]
    tile = slab // PLACES
    columns = head_count
    scale = math.log2(math.e) / math.sqrt(size)

    seq, head = lax.axis_index("seq"), lax.axis_index("head")
    pair, low = seq // 2, seq % 2
    high, core = head // 2, head % 2
    here = high * 2 + low
    mine = pair * 2 + core
    is_self = low == core

    def at(z, of_core):
        return (pair * 2 + z % 2, (z // 2) * 2 + of_core)

    def beside(step):
        other = (mine + step + seq_count) % seq_count
        return ((other // 2) * 2 + low, high * 2 + other % 2)

    outside = beside(2 * core - 1)

    smalls = [
        pltpu.make_async_copy(src, dst, small_sem.at[n])
        for n, (src, dst) in enumerate(((keep_ref, keep_buf), (time_ref, time_buf), (width_ref, width_buf)))
    ]
    for copy in smalls:
        copy.start()

    barrier = pltpu.get_barrier_semaphore()
    pl.semaphore_signal(barrier, inc=1, device_id=at(here, 1 - core), device_id_type=MESH)
    pl.semaphore_signal(barrier, inc=1, device_id=outside, device_id_type=MESH)

    def greet(step, carry):
        z = (here + step) % columns
        for of_core in range(2):
            pl.semaphore_signal(barrier, inc=1, device_id=at(z, of_core), device_id_type=MESH)
        return carry

    lax.fori_loop(1, columns, greet, 0)
    for copy in smalls:
        copy.wait()
    aux_ref[0:group_heads, :] = keep_buf[...].astype(jnp.float32) * (10.0 / 9.0)
    for i in range(PLACES):
        for j in range(TILES):
            offset, place = j // PLACES - 1, j % PLACES
            near = jnp.logical_and(abs(offset) <= time_buf[i], abs(place - i) <= width_buf[i])
            inside = jnp.logical_and(seq + offset >= 0, seq + offset < seq_count)
            penalty = jnp.where(jnp.logical_and(near, inside), 0.0, PENALTY).astype(jnp.float32)
            aux_ref[group_heads + i:group_heads + i + 1, j * 128:(j + 1) * 128] = jnp.full((1, 128), penalty)

    pl.semaphore_wait(barrier, 2 * columns)

    def aux_remote():
        return pltpu.make_async_remote_copy(
            src_ref=aux_ref, dst_ref=aux_buf, send_sem=aux_send, recv_sem=aux_recv,
            device_id=(pair * 2 + core, high * 2 + low), device_id_type=MESH,
        )

    @pl.when(is_self)
    def _():
        pltpu.make_async_copy(aux_ref, aux_buf, aux_recv).start()

    @pl.when(jnp.logical_not(is_self))
    def _():
        aux_remote().start()

    streams = ((k_ref, k_buf, 1), (v_ref, v_buf, 1), (q_ref, q_buf, 0))

    def landing(buf, offset, h):
        return buf.at[h, pl.ds(offset * slab, slab), :]

    def source(ref, z, h):
        return ref.at[:, pl.ds(pl.multiple_of((z * group_heads + h) * size, size), size)]

    def target(buf, offset, h):
        return buf.at[h, pl.ds(pl.multiple_of(offset * slab + head * rows, 16), rows), :]

    def send_head(h, carry):
        for t, (ref, buf, offset) in enumerate(streams):
            def send_to(step, inner, t=t, ref=ref, buf=buf, offset=offset):
                half = (step + 1) // 2
                z = (here + jnp.where(step % 2 == 1, half, columns - half)) % columns
                pltpu.make_async_remote_copy(
                    src_ref=source(ref, z, h), dst_ref=target(buf, offset, h),
                    send_sem=send_sem.at[t], recv_sem=recv_sem.at[t, h],
                    device_id=at(z, low), device_id_type=MESH,
                ).start()
                return inner

            lax.fori_loop(1, columns, send_to, 0)

            @pl.when(is_self)
            def _(t=t, ref=ref, buf=buf, offset=offset):
                pltpu.make_async_copy(source(ref, here, h), target(buf, offset, h), recv_sem.at[t, h]).start()

            @pl.when(jnp.logical_not(is_self))
            def _(t=t, ref=ref, buf=buf, offset=offset):
                pltpu.make_async_remote_copy(
                    src_ref=source(ref, here, h), dst_ref=target(buf, offset, h),
                    send_sem=near_sem.at[t], recv_sem=recv_sem.at[t, h],
                    device_id=at(here, low), device_id_type=MESH,
                ).start()
        return carry

    lax.fori_loop(0, group_heads, send_head, 0)

    def wait_for(ref, sem):
        pltpu.make_async_copy(ref, ref, sem).wait()

    def halo(t, side, h):
        buf = (k_buf, v_buf)[t]
        step = (-1, 1)[side]
        return pltpu.make_async_remote_copy(
            src_ref=landing(buf, 1, h), dst_ref=landing(buf, 1 - step, h),
            send_sem=halo_send.at[t, side, h], recv_sem=halo_recv.at[t, side, h],
            device_id=beside(step), device_id_type=MESH,
        )

    def take_head(h):
        for t, buf in enumerate((k_buf, v_buf)):
            wait_for(landing(buf, 1, h), recv_sem.at[t, h])
            for side in range(2):
                halo(t, side, h).start()

    def out_target(h):
        return o_ref.at[:, pl.ds(pl.multiple_of((here * group_heads + h) * size, size), size)]

    def send_out(h, block):
        src = o_buf.at[h, pl.ds(block * rows, rows), :]
        away = jnp.logical_or(core * columns + block != low * columns + head, False)

        @pl.when(jnp.logical_not(away))
        def _():
            pltpu.make_async_copy(src, out_target(h), out_recv).start()

        @pl.when(jnp.logical_and(away, block // 2 == high))
        def _():
            pltpu.make_async_remote_copy(
                src_ref=src, dst_ref=out_target(h), send_sem=out_near, recv_sem=out_recv,
                device_id=(pair * 2 + core, block), device_id_type=MESH,
            ).start()

        @pl.when(jnp.logical_and(away, block // 2 != high))
        def _():
            pltpu.make_async_remote_copy(
                src_ref=src, dst_ref=out_target(h), send_sem=out_send, recv_sem=out_recv,
                device_id=(pair * 2 + core, block), device_id_type=MESH,
            ).start()

    def attend(h, i):
        q = q_buf[h, i * tile:(i + 1) * tile, :]
        highest = jnp.full((tile, 128), -PENALTY, jnp.float32)
        for j in range(TILES):
            s = lax.dot_general(
                q, k_buf[h, j * tile:(j + 1) * tile, :], (((1,), (1,)), ((), ())),
                preferred_element_type=jnp.float32,
            )
            s_buf[:, j * tile:(j + 1) * tile] = s
            top = s[:, :128]
            for b in range(1, tile // 128):
                top = jnp.maximum(top, s[:, b * 128:(b + 1) * 128])
            highest = jnp.maximum(highest, top - aux_buf[group_heads + i:group_heads + i + 1, j * 128:(j + 1) * 128])
        highest = jnp.max(highest, axis=1, keepdims=True) * scale
        total = jnp.zeros((tile, 128), jnp.float32)
        for j in range(TILES):
            level = highest + aux_buf[group_heads + i:group_heads + i + 1, j * 128:(j + 1) * 128]
            for b in range(j * tile // 128, (j + 1) * tile // 128):
                w = jnp.exp2(s_buf[:, b * 128:(b + 1) * 128] * scale - level)
                total = total + w
                p_buf[:, b * 128:(b + 1) * 128] = w.astype(jnp.bfloat16)
        summed = jnp.dot(p_buf[...], v_buf[h], preferred_element_type=jnp.float32)
        total = jnp.sum(total, axis=1, keepdims=True)
        return summed, total

    def work_head(h):
        for t, buf in enumerate((k_buf, v_buf)):
            for side in range(2):
                halo(t, side, h).wait_recv()
        wait_for(landing(q_buf, 0, h), recv_sem.at[2, h])
        done = 0
        for i in range(PLACES):
            if compute:
                summed, total = attend(h, i)
                keep = aux_buf[pl.ds(h, 1), i * tile:(i + 1) * tile]
                keep = jnp.transpose(jnp.broadcast_to(keep, (8, tile)))[:, :1]
                o_buf[h, i * tile:(i + 1) * tile, :] = (summed * (keep / total)).astype(jnp.bfloat16)
            else:
                o_buf[h, i * tile:(i + 1) * tile, :] = q_buf[h, i * tile:(i + 1) * tile, :]
            ready = (i + 1) * tile // rows
            for block in range(done, ready):
                send_out(h, block)
            done = ready

    take_head(0)
    wait_for(aux_buf, aux_recv)

    def step(h, carry):
        take_head(h)
        work_head(h - 1)
        return carry

    lax.fori_loop(1, group_heads, step, 0)
    work_head(group_heads - 1)

    wait_for(o_ref, out_recv)
    far = (columns - 1) * group_heads * size
    near = group_heads * size
    for t, (ref, _, _) in enumerate(streams):
        wait_for(ref.at[:, :far], send_sem.at[t])

    @pl.when(jnp.logical_not(is_self))
    def _():
        aux_remote().wait_send()
        for t, (ref, _, _) in enumerate(streams):
            wait_for(ref.at[:, :near], near_sem.at[t])

    def settle(h, carry):
        for t in range(2):
            for side in range(2):
                halo(t, side, h).wait_send()
        return carry

    lax.fori_loop(0, group_heads, settle, 0)
    away_rows = (columns - 2) * rows
    wait_for(o_buf.at[:, pl.ds(0, away_rows), :], out_send)

    @pl.when(is_self)
    def _():
        wait_for(o_buf.at[:, pl.ds(0, rows), :], out_near)

    @pl.when(jnp.logical_not(is_self))
    def _():
        wait_for(o_buf.at[:, pl.ds(0, 2 * rows), :], out_near)


def on_device(compute, queries, key_vectors, value_vectors, reach_time, reach_width, keep_mask):
    seq_count, head_count = lax.axis_size("seq"), lax.axis_size("head")
    rows, width = queries.shape
    slab, group_heads = keep_mask.shape
    size = width // (group_heads * head_count)
    tile = slab // PLACES
    aux_shape = (group_heads + PLACES, max(slab, TILES * 128))
    hbm = pl.BlockSpec(memory_space=pltpu.HBM)
    dma = pltpu.SemaphoreType.DMA
    bf16 = jnp.bfloat16
    return pl.pallas_call(
        functools.partial(kernel, group_heads, seq_count, head_count, compute),
        out_shape=jax.ShapeDtypeStruct((rows, width), bf16),
        in_specs=[hbm] * 6,
        out_specs=pl.BlockSpec(memory_space=pltpu.VMEM),
        scratch_shapes=[
            pltpu.VMEM((group_heads, slab, size), bf16),
            pltpu.VMEM((group_heads, 3 * slab, size), bf16),
            pltpu.VMEM((group_heads, 3 * slab, size), bf16),
            pltpu.VMEM((group_heads, slab, size), bf16),
            pltpu.VMEM((tile, 3 * slab), jnp.float32),
            pltpu.VMEM((tile, 3 * slab), bf16),
            pltpu.VMEM(aux_shape, jnp.float32),
            pltpu.VMEM(aux_shape, jnp.float32),
            pltpu.VMEM((group_heads, slab), jnp.int32),
            pltpu.SMEM(reach_time.shape, jnp.int32),
            pltpu.SMEM(reach_width.shape, jnp.int32),
            dma((3,)), dma((3,)), dma((3, group_heads)),
            dma((2, 2, group_heads)), dma((2, 2, group_heads)),
            dma, dma, dma, dma, dma, dma((3,)),
        ],
        compiler_params=pltpu.CompilerParams(
            collective_id=0, has_side_effects=True, vmem_limit_bytes=48 * 1024 * 1024
        ),
    )(*(pltpu.with_memory_space_constraint(x, pltpu.HBM) for x in (keep_mask.T, reach_time, reach_width, queries, key_vectors, value_vectors)))


def solution(mesh, compute=True):
    return jax.shard_map(
        functools.partial(on_device, compute),
        mesh=mesh,
        in_specs=(
            P(("seq", "head"), None),
            P(("seq", "head"), None),
            P(("seq", "head"), None),
            P("seq"),
            P("seq"),
            P("seq", "head"),
        ),
        out_specs=P(("seq", "head"), None),
        check_vma=False,
    )
```

```python
import functools
import math

import jax
import jax.numpy as jnp
from jax import lax
from jax.experimental import pallas as pl
from jax.experimental.pallas import tpu as pltpu
from jax.sharding import PartitionSpec as P

MESH = pl.DeviceIdType.MESH
PLACES = 3
TILES = 3 * PLACES
PENALTY = 1e30


def kernel(
    group_heads, seq_count, head_count, compute,
    keep_ref, time_ref, width_ref, q_ref, k_ref, v_ref, o_ref,
    q_buf, k_buf, v_buf, o_buf, s_buf, p_buf, aux_ref, aux_buf,
    keep_buf, time_buf, width_buf,
    send_sem, near_sem, recv_sem, halo_send, halo_recv,
    out_send, out_near, out_recv, aux_send, aux_recv, small_sem,
):
    rows, size = q_ref.shape[0], q_buf.shape[2]
    slab = q_buf.shape[1]
    tile = slab // PLACES
    columns = head_count
    scale = math.log2(math.e) / math.sqrt(size)

    seq, head = lax.axis_index("seq"), lax.axis_index("head")
    pair, low = seq // 2, seq % 2
    high, core = head // 2, head % 2
    here = high * 2 + low
    mine = pair * 2 + core
    is_self = low == core

    def at(z, of_core):
        return (pair * 2 + z % 2, (z // 2) * 2 + of_core)

    def beside(step):
        other = (mine + step + seq_count) % seq_count
        return ((other // 2) * 2 + low, high * 2 + other % 2)

    outside = beside(2 * core - 1)

    smalls = [
        pltpu.make_async_copy(src, dst, small_sem.at[n])
        for n, (src, dst) in enumerate(((keep_ref, keep_buf), (time_ref, time_buf), (width_ref, width_buf)))
    ]
    for copy in smalls:
        copy.start()

    barrier = pltpu.get_barrier_semaphore()
    pl.semaphore_signal(barrier, inc=1, device_id=at(here, 1 - core), device_id_type=MESH)
    pl.semaphore_signal(barrier, inc=1, device_id=outside, device_id_type=MESH)

    def greet(step, carry):
        z = (here + step) % columns
        for of_core in range(2):
            pl.semaphore_signal(barrier, inc=1, device_id=at(z, of_core), device_id_type=MESH)
        return carry

    lax.fori_loop(1, columns, greet, 0)
    pl.semaphore_wait(barrier, 2 * columns)

    def aux_remote():
        return pltpu.make_async_remote_copy(
            src_ref=aux_ref, dst_ref=aux_buf, send_sem=aux_send, recv_sem=aux_recv,
            device_id=(pair * 2 + core, high * 2 + low), device_id_type=MESH,
        )

    streams = ((k_ref, k_buf, 1), (v_ref, v_buf, 1), (q_ref, q_buf, 0))

    def landing(buf, offset, h):
        return buf.at[h, pl.ds(offset * slab, slab), :]

    def source(ref, z, h):
        return ref.at[:, pl.ds(pl.multiple_of((z * group_heads + h) * size, size), size)]

    def target(buf, offset, h):
        return buf.at[h, pl.ds(pl.multiple_of(offset * slab + head * rows, 16), rows), :]

    def send(t, h):
        ref, buf, offset = streams[t]

        def send_to(step, carry):
            half = (step + 1) // 2
            z = (here + jnp.where(step % 2 == 1, half, columns - half)) % columns
            pltpu.make_async_remote_copy(
                src_ref=source(ref, z, h), dst_ref=target(buf, offset, h),
                send_sem=send_sem.at[t], recv_sem=recv_sem.at[t, h],
                device_id=at(z, low), device_id_type=MESH,
            ).start()
            return carry

        lax.fori_loop(1, columns, send_to, 0)

        @pl.when(is_self)
        def _():
            pltpu.make_async_copy(source(ref, here, h), target(buf, offset, h), recv_sem.at[t, h]).start()

        @pl.when(jnp.logical_not(is_self))
        def _():
            pltpu.make_async_remote_copy(
                src_ref=source(ref, here, h), dst_ref=target(buf, offset, h),
                send_sem=near_sem.at[t], recv_sem=recv_sem.at[t, h],
                device_id=at(here, low), device_id_type=MESH,
            ).start()

    def send_heads(h, carry):
        send(0, h)
        send(1, h)
        send(2, h)
        return carry

    send(0, 0)
    send(1, 0)
    for copy in smalls:
        copy.wait()
    aux_ref[0:group_heads, :] = keep_buf[...].astype(jnp.float32) * (10.0 / 9.0)
    for i in range(PLACES):
        for j in range(TILES):
            offset, place = j // PLACES - 1, j % PLACES
            near = jnp.logical_and(abs(offset) <= time_buf[i], abs(place - i) <= width_buf[i])
            inside = jnp.logical_and(seq + offset >= 0, seq + offset < seq_count)
            penalty = jnp.where(jnp.logical_and(near, inside), 0.0, PENALTY).astype(jnp.float32)
            aux_ref[group_heads + i:group_heads + i + 1, j * 128:(j + 1) * 128] = jnp.full((1, 128), penalty)

    @pl.when(is_self)
    def _():
        pltpu.make_async_copy(aux_ref, aux_buf, aux_recv).start()

    @pl.when(jnp.logical_not(is_self))
    def _():
        aux_remote().start()

    send(2, 0)
    lax.fori_loop(1, group_heads, send_heads, 0)

    def wait_for(ref, sem):
        pltpu.make_async_copy(ref, ref, sem).wait()

    def halo(t, side, h):
        buf = (k_buf, v_buf)[t]
        step = (-1, 1)[side]
        return pltpu.make_async_remote_copy(
            src_ref=landing(buf, 1, h), dst_ref=landing(buf, 1 - step, h),
            send_sem=halo_send.at[t, side, h], recv_sem=halo_recv.at[t, side, h],
            device_id=beside(step), device_id_type=MESH,
        )

    def take_head(h):
        for t, buf in enumerate((k_buf, v_buf)):
            wait_for(landing(buf, 1, h), recv_sem.at[t, h])
            for side in range(2):
                halo(t, side, h).start()

    def out_target(h):
        return o_ref.at[:, pl.ds(pl.multiple_of((here * group_heads + h) * size, size), size)]

    def send_out(h, block):
        src = o_buf.at[h, pl.ds(pl.multiple_of(block * rows, 16), rows), :]
        away = core * columns + block != low * columns + head

        @pl.when(jnp.logical_not(away))
        def _():
            pltpu.make_async_copy(src, out_target(h), out_recv).start()

        @pl.when(jnp.logical_and(away, block // 2 == high))
        def _():
            pltpu.make_async_remote_copy(
                src_ref=src, dst_ref=out_target(h), send_sem=out_near, recv_sem=out_recv,
                device_id=(pair * 2 + core, block), device_id_type=MESH,
            ).start()

        @pl.when(jnp.logical_and(away, block // 2 != high))
        def _():
            pltpu.make_async_remote_copy(
                src_ref=src, dst_ref=out_target(h), send_sem=out_send, recv_sem=out_recv,
                device_id=(pair * 2 + core, block), device_id_type=MESH,
            ).start()

    def attend(h, i):
        q = q_buf[h, i * tile:(i + 1) * tile, :]
        highest = jnp.full((tile, 128), -PENALTY, jnp.float32)
        for j in range(TILES):
            s = lax.dot_general(
                q, k_buf[h, j * tile:(j + 1) * tile, :], (((1,), (1,)), ((), ())),
                preferred_element_type=jnp.float32,
            )
            s_buf[:, j * tile:(j + 1) * tile] = s
            top = s[:, :128]
            for b in range(1, tile // 128):
                top = jnp.maximum(top, s[:, b * 128:(b + 1) * 128])
            highest = jnp.maximum(highest, top - aux_buf[group_heads + i:group_heads + i + 1, j * 128:(j + 1) * 128])
        highest = jnp.max(highest, axis=1, keepdims=True) * scale
        total = jnp.zeros((tile, 128), jnp.float32)
        for j in range(TILES):
            level = highest + aux_buf[group_heads + i:group_heads + i + 1, j * 128:(j + 1) * 128]
            for b in range(j * tile // 128, (j + 1) * tile // 128):
                w = jnp.exp2(s_buf[:, b * 128:(b + 1) * 128] * scale - level)
                total = total + w
                p_buf[:, b * 128:(b + 1) * 128] = w.astype(jnp.bfloat16)
        summed = jnp.dot(p_buf[...], v_buf[h], preferred_element_type=jnp.float32)
        total = jnp.sum(total, axis=1, keepdims=True)
        return summed, total

    def work_head(h, last=False):
        for t, buf in enumerate((k_buf, v_buf)):
            for side in range(2):
                halo(t, side, h).wait_recv()
        wait_for(landing(q_buf, 0, h), recv_sem.at[2, h])
        done = 0
        for i in range(PLACES):
            if compute:
                summed, total = attend(h, i)
                keep = aux_buf[pl.ds(h, 1), i * tile:(i + 1) * tile]
                keep = jnp.transpose(jnp.broadcast_to(keep, (8, tile)))[:, :1]
                o_buf[h, i * tile:(i + 1) * tile, :] = (summed * (keep / total)).astype(jnp.bfloat16)
            else:
                o_buf[h, i * tile:(i + 1) * tile, :] = q_buf[h, i * tile:(i + 1) * tile, :]
            if last:
                ready = (i + 1) * tile // rows
                for block in ((1, 0), (3, 2, 4), (5, 7, 6))[i]:
                    send_out(h, block)
                done = ready
        if not last:
            def send_rest(step, carry):
                send_out(h, step + 1 - 2 * (step % 2))
                return carry

            lax.fori_loop(0, columns, send_rest, 0)

    take_head(0)
    wait_for(aux_buf, aux_recv)

    def step(h, carry):
        take_head(h)
        work_head(h - 1)
        return carry

    lax.fori_loop(1, group_heads, step, 0)
    work_head(group_heads - 1, last=True)

    wait_for(o_ref, out_recv)
    far = (columns - 1) * group_heads * size
    near = group_heads * size
    for t, (ref, _, _) in enumerate(streams):
        wait_for(ref.at[:, :far], send_sem.at[t])

    @pl.when(jnp.logical_not(is_self))
    def _():
        aux_remote().wait_send()
        for t, (ref, _, _) in enumerate(streams):
            wait_for(ref.at[:, :near], near_sem.at[t])

    def settle(h, carry):
        for t in range(2):
            for side in range(2):
                halo(t, side, h).wait_send()
        return carry

    lax.fori_loop(0, group_heads, settle, 0)
    away_rows = (columns - 2) * rows
    wait_for(o_buf.at[:, pl.ds(0, away_rows), :], out_send)

    @pl.when(is_self)
    def _():
        wait_for(o_buf.at[:, pl.ds(0, rows), :], out_near)

    @pl.when(jnp.logical_not(is_self))
    def _():
        wait_for(o_buf.at[:, pl.ds(0, 2 * rows), :], out_near)


def on_device(compute, queries, key_vectors, value_vectors, reach_time, reach_width, keep_mask):
    seq_count, head_count = lax.axis_size("seq"), lax.axis_size("head")
    rows, width = queries.shape
    slab, group_heads = keep_mask.shape
    size = width // (group_heads * head_count)
    tile = slab // PLACES
    aux_shape = (group_heads + PLACES, max(slab, TILES * 128))
    hbm = pl.BlockSpec(memory_space=pltpu.HBM)
    dma = pltpu.SemaphoreType.DMA
    bf16 = jnp.bfloat16
    return pl.pallas_call(
        functools.partial(kernel, group_heads, seq_count, head_count, compute),
        out_shape=jax.ShapeDtypeStruct((rows, width), bf16),
        in_specs=[hbm] * 6,
        out_specs=pl.BlockSpec(memory_space=pltpu.VMEM),
        scratch_shapes=[
            pltpu.VMEM((group_heads, slab, size), bf16),
            pltpu.VMEM((group_heads, 3 * slab, size), bf16),
            pltpu.VMEM((group_heads, 3 * slab, size), bf16),
            pltpu.VMEM((group_heads, slab, size), bf16),
            pltpu.VMEM((tile, 3 * slab), jnp.float32),
            pltpu.VMEM((tile, 3 * slab), bf16),
            pltpu.VMEM(aux_shape, jnp.float32),
            pltpu.VMEM(aux_shape, jnp.float32),
            pltpu.VMEM((group_heads, slab), jnp.int32),
            pltpu.SMEM(reach_time.shape, jnp.int32),
            pltpu.SMEM(reach_width.shape, jnp.int32),
            dma((3,)), dma((3,)), dma((3, group_heads)),
            dma((2, 2, group_heads)), dma((2, 2, group_heads)),
            dma, dma, dma, dma, dma, dma((3,)),
        ],
        compiler_params=pltpu.CompilerParams(
            collective_id=0, has_side_effects=True, vmem_limit_bytes=48 * 1024 * 1024
        ),
    )(*(pltpu.with_memory_space_constraint(x, pltpu.HBM) for x in (keep_mask.T, reach_time, reach_width, queries, key_vectors, value_vectors)))


def solution(mesh, compute=True):
    return jax.shard_map(
        functools.partial(on_device, compute),
        mesh=mesh,
        in_specs=(
            P(("seq", "head"), None),
            P(("seq", "head"), None),
            P(("seq", "head"), None),
            P("seq"),
            P("seq"),
            P("seq", "head"),
        ),
        out_specs=P(("seq", "head"), None),
        check_vma=False,
    )
```

```python
import functools
import math

import jax
import jax.numpy as jnp
from jax import lax
from jax.experimental import pallas as pl
from jax.experimental.pallas import tpu as pltpu
from jax.sharding import PartitionSpec as P

MESH = pl.DeviceIdType.MESH
PLACES = 3
TILES = 3 * PLACES
PENALTY = 1e30


def kernel(
    group_heads, seq_count, head_count, compute,
    keep_ref, time_ref, width_ref, q_ref, k_ref, v_ref, o_ref,
    q_buf, k_buf, v_buf, o_buf, s_buf, p_buf, aux_ref, aux_buf,
    keep_buf, time_buf, width_buf,
    send_sem, near_sem, recv_sem, halo_send, halo_recv,
    out_send, out_near, out_recv, aux_send, aux_recv, small_sem,
):
    rows, size = q_ref.shape[0], q_buf.shape[2]
    slab = q_buf.shape[1]
    tile = slab // PLACES
    columns = head_count
    scale = math.log2(math.e) / math.sqrt(size)

    seq, head = lax.axis_index("seq"), lax.axis_index("head")
    pair, low = seq // 2, seq % 2
    high, core = head // 2, head % 2
    here = high * 2 + low
    mine = pair * 2 + core
    is_self = low == core

    def at(z, of_core):
        return (pair * 2 + z % 2, (z // 2) * 2 + of_core)

    def beside(step):
        other = (mine + step + seq_count) % seq_count
        return ((other // 2) * 2 + low, high * 2 + other % 2)

    outside = beside(2 * core - 1)

    barrier = pltpu.get_barrier_semaphore()
    pl.semaphore_signal(barrier, inc=1, device_id=at(here, 1 - core), device_id_type=MESH)
    pl.semaphore_signal(barrier, inc=1, device_id=outside, device_id_type=MESH)

    def greet(step, carry):
        z = (here + step) % columns
        for of_core in range(2):
            pl.semaphore_signal(barrier, inc=1, device_id=at(z, of_core), device_id_type=MESH)
        return carry

    lax.fori_loop(1, columns, greet, 0)
    smalls = [
        pltpu.make_async_copy(src, dst, small_sem.at[n])
        for n, (src, dst) in enumerate(((keep_ref, keep_buf), (time_ref, time_buf), (width_ref, width_buf)))
    ]
    for copy in smalls:
        copy.start()

    pl.semaphore_wait(barrier, 2 * columns)

    def aux_remote():
        return pltpu.make_async_remote_copy(
            src_ref=aux_ref, dst_ref=aux_buf, send_sem=aux_send, recv_sem=aux_recv,
            device_id=(pair * 2 + core, high * 2 + low), device_id_type=MESH,
        )

    streams = ((k_ref, k_buf, 1), (v_ref, v_buf, 1), (q_ref, q_buf, 0))

    def landing(buf, offset, h):
        return buf.at[h, pl.ds(offset * slab, slab), :]

    def source(ref, z, h):
        return ref.at[:, pl.ds(pl.multiple_of((z * group_heads + h) * size, size), size)]

    def target(buf, offset, h):
        return buf.at[h, pl.ds(pl.multiple_of(offset * slab + head * rows, 16), rows), :]

    def send(t, h):
        ref, buf, offset = streams[t]

        def send_to(step, carry):
            half = (step + 1) // 2
            z = (here + jnp.where(step % 2 == 1, half, columns - half)) % columns
            pltpu.make_async_remote_copy(
                src_ref=source(ref, z, h), dst_ref=target(buf, offset, h),
                send_sem=send_sem.at[t], recv_sem=recv_sem.at[t, h],
                device_id=at(z, low), device_id_type=MESH,
            ).start()
            return carry

        lax.fori_loop(1, columns, send_to, 0)

        @pl.when(is_self)
        def _():
            pltpu.make_async_copy(source(ref, here, h), target(buf, offset, h), recv_sem.at[t, h]).start()

        @pl.when(jnp.logical_not(is_self))
        def _():
            pltpu.make_async_remote_copy(
                src_ref=source(ref, here, h), dst_ref=target(buf, offset, h),
                send_sem=near_sem.at[t], recv_sem=recv_sem.at[t, h],
                device_id=at(here, low), device_id_type=MESH,
            ).start()

    def send_heads(h, carry):
        send(0, h)
        send(1, h)
        send(2, h)
        return carry

    send(0, 0)
    send(1, 0)
    for copy in smalls:
        copy.wait()
    aux_ref[0:group_heads, :] = keep_buf[...].astype(jnp.float32) * (10.0 / 9.0)
    for i in range(PLACES):
        for j in range(TILES):
            offset, place = j // PLACES - 1, j % PLACES
            near = jnp.logical_and(abs(offset) <= time_buf[i], abs(place - i) <= width_buf[i])
            inside = jnp.logical_and(seq + offset >= 0, seq + offset < seq_count)
            penalty = jnp.where(jnp.logical_and(near, inside), 0.0, PENALTY).astype(jnp.float32)
            aux_ref[group_heads + i:group_heads + i + 1, j * 128:(j + 1) * 128] = jnp.full((1, 128), penalty)

    @pl.when(is_self)
    def _():
        pltpu.make_async_copy(aux_ref, aux_buf, aux_recv).start()

    @pl.when(jnp.logical_not(is_self))
    def _():
        aux_remote().start()

    send(2, 0)
    lax.fori_loop(1, group_heads, send_heads, 0)

    def wait_for(ref, sem):
        pltpu.make_async_copy(ref, ref, sem).wait()

    def halo(t, side, h):
        buf = (k_buf, v_buf)[t]
        step = (-1, 1)[side]
        return pltpu.make_async_remote_copy(
            src_ref=landing(buf, 1, h), dst_ref=landing(buf, 1 - step, h),
            send_sem=halo_send.at[t, side, h], recv_sem=halo_recv.at[t, side, h],
            device_id=beside(step), device_id_type=MESH,
        )

    def take_head(h):
        for t, buf in enumerate((k_buf, v_buf)):
            wait_for(landing(buf, 1, h), recv_sem.at[t, h])
            for side in range(2):
                halo(t, side, h).start()

    def out_target(h):
        return o_ref.at[:, pl.ds(pl.multiple_of((here * group_heads + h) * size, size), size)]

    def send_out(h, block):
        src = o_buf.at[h, pl.ds(pl.multiple_of(block * rows, 16), rows), :]
        away = core * columns + block != low * columns + head

        @pl.when(jnp.logical_not(away))
        def _():
            pltpu.make_async_copy(src, out_target(h), out_recv).start()

        @pl.when(jnp.logical_and(away, block // 2 == high))
        def _():
            pltpu.make_async_remote_copy(
                src_ref=src, dst_ref=out_target(h), send_sem=out_near, recv_sem=out_recv,
                device_id=(pair * 2 + core, block), device_id_type=MESH,
            ).start()

        @pl.when(jnp.logical_and(away, block // 2 != high))
        def _():
            pltpu.make_async_remote_copy(
                src_ref=src, dst_ref=out_target(h), send_sem=out_send, recv_sem=out_recv,
                device_id=(pair * 2 + core, block), device_id_type=MESH,
            ).start()

    def attend(h, i):
        q = q_buf[h, i * tile:(i + 1) * tile, :]
        highest = jnp.full((tile, 128), -PENALTY, jnp.float32)
        for j in range(TILES):
            s = lax.dot_general(
                q, k_buf[h, j * tile:(j + 1) * tile, :], (((1,), (1,)), ((), ())),
                preferred_element_type=jnp.float32,
            )
            s_buf[:, j * tile:(j + 1) * tile] = s
            top = s[:, :128]
            for b in range(1, tile // 128):
                top = jnp.maximum(top, s[:, b * 128:(b + 1) * 128])
            highest = jnp.maximum(highest, top - aux_buf[group_heads + i:group_heads + i + 1, j * 128:(j + 1) * 128])
        highest = jnp.max(highest, axis=1, keepdims=True) * scale
        total = jnp.zeros((tile, 128), jnp.float32)
        for j in range(TILES):
            level = highest + aux_buf[group_heads + i:group_heads + i + 1, j * 128:(j + 1) * 128]
            for b in range(j * tile // 128, (j + 1) * tile // 128):
                w = jnp.exp2(s_buf[:, b * 128:(b + 1) * 128] * scale - level)
                total = total + w
                p_buf[:, b * 128:(b + 1) * 128] = w.astype(jnp.bfloat16)
        summed = jnp.dot(p_buf[...], v_buf[h], preferred_element_type=jnp.float32)
        total = jnp.sum(total, axis=1, keepdims=True)
        return summed, total

    def work_head(h, last=False):
        for t, buf in enumerate((k_buf, v_buf)):
            for side in range(2):
                halo(t, side, h).wait_recv()
        wait_for(landing(q_buf, 0, h), recv_sem.at[2, h])
        done = 0
        for i in range(PLACES):
            if compute:
                summed, total = attend(h, i)
                keep = aux_buf[pl.ds(h, 1), i * tile:(i + 1) * tile]
                keep = jnp.transpose(jnp.broadcast_to(keep, (8, tile)))[:, :1]
                o_buf[h, i * tile:(i + 1) * tile, :] = (summed * (keep / total)).astype(jnp.bfloat16)
            else:
                o_buf[h, i * tile:(i + 1) * tile, :] = q_buf[h, i * tile:(i + 1) * tile, :]
            if last:
                ready = (i + 1) * tile // rows
                for block in ((1, 0), (3, 2, 4), (5, 7, 6))[i]:
                    send_out(h, block)
                done = ready
        if not last:
            def send_rest(step, carry):
                send_out(h, (step // 2) * 2 + (step + h + 1) % 2)
                return carry

            lax.fori_loop(0, columns, send_rest, 0)

    take_head(0)
    wait_for(aux_buf, aux_recv)

    def step(h, carry):
        take_head(h)
        work_head(h - 1)
        return carry

    lax.fori_loop(1, group_heads, step, 0)
    work_head(group_heads - 1, last=True)

    wait_for(o_ref, out_recv)
    far = (columns - 1) * group_heads * size
    near = group_heads * size
    for t, (ref, _, _) in enumerate(streams):
        wait_for(ref.at[:, :far], send_sem.at[t])

    @pl.when(jnp.logical_not(is_self))
    def _():
        aux_remote().wait_send()
        for t, (ref, _, _) in enumerate(streams):
            wait_for(ref.at[:, :near], near_sem.at[t])

    def settle(h, carry):
        for t in range(2):
            for side in range(2):
                halo(t, side, h).wait_send()
        return carry

    lax.fori_loop(0, group_heads, settle, 0)
    away_rows = (columns - 2) * rows
    wait_for(o_buf.at[:, pl.ds(0, away_rows), :], out_send)

    @pl.when(is_self)
    def _():
        wait_for(o_buf.at[:, pl.ds(0, rows), :], out_near)

    @pl.when(jnp.logical_not(is_self))
    def _():
        wait_for(o_buf.at[:, pl.ds(0, 2 * rows), :], out_near)


def on_device(compute, queries, key_vectors, value_vectors, reach_time, reach_width, keep_mask):
    seq_count, head_count = lax.axis_size("seq"), lax.axis_size("head")
    rows, width = queries.shape
    slab, group_heads = keep_mask.shape
    size = width // (group_heads * head_count)
    tile = slab // PLACES
    aux_shape = (group_heads + PLACES, max(slab, TILES * 128))
    hbm = pl.BlockSpec(memory_space=pltpu.HBM)
    dma = pltpu.SemaphoreType.DMA
    bf16 = jnp.bfloat16
    return pl.pallas_call(
        functools.partial(kernel, group_heads, seq_count, head_count, compute),
        out_shape=jax.ShapeDtypeStruct((rows, width), bf16),
        in_specs=[hbm] * 6,
        out_specs=pl.BlockSpec(memory_space=pltpu.VMEM),
        scratch_shapes=[
            pltpu.VMEM((group_heads, slab, size), bf16),
            pltpu.VMEM((group_heads, 3 * slab, size), bf16),
            pltpu.VMEM((group_heads, 3 * slab, size), bf16),
            pltpu.VMEM((group_heads, slab, size), bf16),
            pltpu.VMEM((tile, 3 * slab), jnp.float32),
            pltpu.VMEM((tile, 3 * slab), bf16),
            pltpu.VMEM(aux_shape, jnp.float32),
            pltpu.VMEM(aux_shape, jnp.float32),
            pltpu.VMEM((group_heads, slab), jnp.int32),
            pltpu.SMEM(reach_time.shape, jnp.int32),
            pltpu.SMEM(reach_width.shape, jnp.int32),
            dma((3,)), dma((3,)), dma((3, group_heads)),
            dma((2, 2, group_heads)), dma((2, 2, group_heads)),
            dma, dma, dma, dma, dma, dma((3,)),
        ],
        compiler_params=pltpu.CompilerParams(
            collective_id=0, has_side_effects=True, vmem_limit_bytes=48 * 1024 * 1024
        ),
    )(*(pltpu.with_memory_space_constraint(x, pltpu.HBM) for x in (keep_mask.T, reach_time, reach_width, queries, key_vectors, value_vectors)))


def solution(mesh, compute=True):
    return jax.shard_map(
        functools.partial(on_device, compute),
        mesh=mesh,
        in_specs=(
            P(("seq", "head"), None),
            P(("seq", "head"), None),
            P(("seq", "head"), None),
            P("seq"),
            P("seq"),
            P("seq", "head"),
        ),
        out_specs=P(("seq", "head"), None),
        check_vma=False,
    )
```
